512 devices in a mesh: rep: 8 (over y), exp: 64 (over x, z, core).
Axes of the slice: x: 4, y: 8, z: 8, core: 2. Of those that a mesh axis runs over, the one named last changes fastest.
Arguments:
- tokens: bfloat16 [65536, 1024], P(('rep', 'exp')), may hold values from -6 to 6
- cotangent: bfloat16 [65536, 1024], P(('rep', 'exp')), may hold values from -6 to 6
- expert_ids: int32 [65536, 2], P(('rep', 'exp')), may hold values from 0 to 63, all different within a row; in each aligned block of 128 rows (0 to 127, 128 to 255, ...) at most 8 rows name the same one
- combine_weight: float32 [65536, 2], P(('rep', 'exp')), may hold values from 0.2 to 1
- gate_weight: bfloat16 [64, 1024, 768], P('exp', 'rep'), may hold values from -0.1875 to 0.1875
- up_weight: bfloat16 [64, 1024, 768], P('exp', 'rep'), may hold values from -0.1875 to 0.1875
- down_weight: bfloat16 [64, 768, 1024], P('exp', None, 'rep'), may hold values from -0.21875 to 0.21875
Outputs:
- mixed: bfloat16 [65536, 1024], P(('rep', 'exp'))
- token_grad: bfloat16 [65536, 1024], P(('rep', 'exp'))
- gate_grad: bfloat16 [64, 1024, 768], P('exp', 'rep')
- up_grad: bfloat16 [64, 1024, 768], P('exp', 'rep')
- down_grad: bfloat16 [64, 768, 1024], P('exp', None, 'rep')
The draws below stay inside these ranges and needn't reach their ends.
Inputs may be any that keep to these rules, and one draw needn't show every extreme that they name: `expert_ids`: each token names 2 different experts. Among the 128 tokens of one aligned block of rows, no expert is named more than 8 times, and in some block an expert is named exactly 8 times.
All inputs are finite; a program needn't handle non-finite values.
Results may differ from the reference program's by a relative error of at most 0.014.
Values may be sent and summed in bfloat16 or wider, within the bound.
No kernel may reach another device: no remote copies, remote signals or barrier semaphores. Data moves between devices by JAX's collectives and lax.ppermute only.
A program may use at most 64 MiB of HBM per device.

```python
import math
import jax
import jax.numpy as jnp
import numpy as np
from jax import lax

D = 1024
FF = 768
TOP = 2
TOK_DEV = 128
EXPERTS = 64
CAP = 8
TOKENS = 65536
N_REP = 8
N_EXP = 64


def levels(stream_key, dims, pieces, smallest, high):
    def one(dim, shards_of):
        heights = jax.random.uniform(jax.random.fold_in(jax.random.fold_in(stream_key, 6), dim), (shards_of,), jnp.float32, smallest / len(pieces), high / len(pieces))
        return jnp.repeat(jnp.exp(heights), dims[dim] // shards_of).reshape((-1,) + (1,) * (len(dims) - dim - 1))

    loudness = one(*pieces[0])
    for cut in pieces[1:]:
        loudness = loudness * one(*cut)
    return loudness


def routed_block(own_key, own, number, rows, count, top, reach, slope):
    ranking = jax.random.permutation(own_key, count)
    packed, common = shares(count, rows * top, reach, slope, True), shares(count, rows * top, reach, slope, False)
    places = jnp.arange(count)

    def named(sizes, offset_by):
        used = int((sizes > 0).sum())
        fixed = max(1, used // 4)
        moved = fixed + (places - fixed + offset_by * (used - fixed)) % max(1, count - fixed)
        return jnp.zeros((count,), jnp.int32).at[ranking[jnp.where(places < fixed, places, moved)]].set(jnp.asarray(sizes, jnp.int32))

    sizes = jnp.where(number % 4 == 0, named(packed, number // 4), named(common, number - number // 4 - 1))
    mixed = jax.random.permutation(jax.random.fold_in(own, 3), count)
    giver, receiver = mixed[0:count // 2 * 2:2], mixed[1:count // 2 * 2:2]
    slack = jnp.minimum(sizes[giver] - 1, reach - sizes[receiver]) // 2
    slack = jnp.where((giver == ranking[0]) | (receiver == ranking[0]) | (sizes[receiver] == 0), 0, jnp.maximum(slack, 0))
    moved = jax.random.randint(jax.random.fold_in(own, 4), (count // 2,), 0, 1 << 20) % (slack + 1)
    sizes = sizes.at[giver].add(-moved).at[receiver].add(moved)
    members = jnp.searchsorted(jnp.cumsum(sizes), jnp.arange(rows * top), side="right").astype(jnp.int32)
    listing = members.reshape(top, rows).T
    listing = listing[jax.random.permutation(jax.random.fold_in(own, 1), rows)]
    offset_by = jax.random.randint(jax.random.fold_in(own, 2), (rows, 1), 0, top)
    return jnp.take_along_axis(listing, (jnp.arange(top)[None, :] + offset_by) % top, axis=1)


def shares(number_of, total, reach, slope, full):
    loads = [(1 << 20) // math.isqrt(rank ** slope) + 1 for rank in range(1, number_of + 1)]
    largest = reach if full else min(reach, max(-(-total // number_of), total * loads[0] // sum(loads)))
    least = 1 if total - largest >= number_of - 1 else 0
    counts, surplus = [largest] + [least] * (number_of - 1), total - largest - least * (number_of - 1)
    while surplus > 0:
        free = [i for i in range(1, number_of) if counts[i] < largest] or [i for i in range(1, number_of) if counts[i] < reach]
        pool, left = sum([loads[i] for i in free]), surplus
        for i in free:
            extra = min(reach - counts[i], max(1, left * loads[i] // pool), surplus)
            counts[i] = counts[i] + extra
            surplus = surplus - extra
    return np.array(counts)


def centred(key, extent, width, most, split=(), kind=jnp.bfloat16):
    values = jax.random.normal(key, extent, jnp.float32) * width
    if len(split) > 0:
        values = levels(key, extent, split, -0.22, 0.18) * values
    return jnp.clip(values, min=-most, max=most).astype(kind)


def setup_inputs(seed: int = 0) -> dict:
    keys = jax.random.split(jax.random.key(seed), 8)
    tokens = centred(keys[0], (TOKENS, D), 1.0, 6.0, ((0, 512),))
    cotangent = centred(keys[1], (TOKENS, D), 1.0, 6.0, ((0, 512),))
    expert_ids_keys = jax.random.split(jax.random.fold_in(keys[2], 1), TOKENS // TOK_DEV)
    expert_ids_turns = jax.random.permutation(jax.random.fold_in(keys[2], 3), TOKENS // TOK_DEV)
    expert_ids = jax.vmap(lambda own, number: routed_block(jax.random.fold_in(keys[2], 2), own, number, TOK_DEV, EXPERTS, TOP, CAP, 2))(expert_ids_keys, expert_ids_turns).reshape((TOKENS, TOP))
    combine_weight = jnp.clip(0.2 + 0.8 * jax.random.uniform(keys[3], (TOKENS, TOP), jnp.float32) ** levels(keys[3], (TOKENS, TOP), ((0, 512),), -0.2, 0.2), 0.2, 1.0)
    gate_weight = centred(keys[4], (EXPERTS, D, FF), D ** -0.5, 0.1875, ((0, 64), (1, 8)))
    up_weight = centred(keys[5], (EXPERTS, D, FF), D ** -0.5, 0.1875, ((0, 64), (1, 8)))
    down_weight = centred(keys[6], (EXPERTS, FF, D), FF ** -0.5, 0.21875, ((0, 64), (2, 8)))
    return dict(tokens=tokens, cotangent=cotangent, expert_ids=expert_ids, combine_weight=combine_weight, gate_weight=gate_weight, up_weight=up_weight, down_weight=down_weight)


def slot_index(block_ids):
    flat = block_ids.reshape(-1).astype(jnp.int32)
    onehot = (flat[:, None] == jnp.arange(EXPERTS, dtype=jnp.int32)[None, :]).astype(jnp.int32)
    before = jnp.cumsum(onehot, axis=0) - onehot
    return (flat * CAP + jnp.sum(before * onehot, axis=1)).astype(jnp.int32)


def reference(tokens, cotangent, expert_ids, combine_weight, gate_weight, up_weight, down_weight):
    devices_all = N_REP * N_EXP
    pair_count = TOK_DEV * TOP
    block_ids = expert_ids.reshape(devices_all, TOK_DEV, TOP)
    destination = jax.vmap(slot_index)(block_ids)
    device_rows = jnp.arange(devices_all, dtype=jnp.int32)[:, None]
    inverse = jnp.full((devices_all, EXPERTS * CAP), pair_count, jnp.int32)
    pair_numbers = jnp.broadcast_to(jnp.arange(pair_count, dtype=jnp.int32)[None, :], (devices_all, pair_count))
    inverse = inverse.at[device_rows, destination].set(pair_numbers)
    token_rows = tokens.reshape(devices_all, TOK_DEV, D)
    zero_row = jnp.zeros((devices_all, 1, D), tokens.dtype)
    x_pairs = jnp.concatenate([jnp.repeat(token_rows, TOP, axis=1), zero_row], axis=1)
    weighted = (combine_weight.reshape(devices_all, TOK_DEV, TOP, 1).astype(jnp.float32)
                * cotangent.reshape(devices_all, TOK_DEV, 1, D).astype(jnp.float32)).astype(jnp.bfloat16)
    c_pairs = jnp.concatenate([weighted.reshape(devices_all, pair_count, D), zero_row.astype(jnp.bfloat16)], axis=1)
    weight_pairs = jnp.concatenate([combine_weight.reshape(devices_all, pair_count).astype(jnp.float32),
                                    jnp.zeros((devices_all, 1), jnp.float32)], axis=1)

    def per_expert(carry, expert):
        out_acc, grad_acc = carry
        index = lax.dynamic_slice_in_dim(inverse, (expert * CAP).astype(jnp.int32), CAP, 1)
        block_x = jnp.take_along_axis(x_pairs, index[:, :, None], axis=1).reshape(devices_all * CAP, D)
        block_c = jnp.take_along_axis(c_pairs, index[:, :, None], axis=1).reshape(devices_all * CAP, D)
        w_gate = gate_weight[expert]
        w_up = up_weight[expert]
        w_down = down_weight[expert]
        gate_value = jnp.dot(block_x, w_gate, preferred_element_type=jnp.float32)
        up_value = jnp.dot(block_x, w_up, preferred_element_type=jnp.float32)
        swish_value = jax.nn.silu(gate_value)
        hidden = (swish_value * up_value).astype(jnp.bfloat16)
        output = jnp.dot(hidden, w_down, preferred_element_type=jnp.float32).astype(jnp.bfloat16)
        grad_hidden = lax.dot_general(block_c, w_down, (((1,), (1,)), ((), ())), preferred_element_type=jnp.float32)
        sigma = jax.nn.sigmoid(gate_value)
        grad_gate = (grad_hidden * up_value * sigma * (1.0 + gate_value * (1.0 - sigma))).astype(jnp.bfloat16)
        grad_up = (grad_hidden * swish_value).astype(jnp.bfloat16)
        grad_rows = (lax.dot_general(grad_gate, w_gate, (((1,), (1,)), ((), ())), preferred_element_type=jnp.float32)
                     + lax.dot_general(grad_up, w_up, (((1,), (1,)), ((), ())), preferred_element_type=jnp.float32)).astype(jnp.bfloat16)
        rep_x = block_x.reshape(N_REP, N_EXP * CAP, D).astype(jnp.float32)
        rep_c = block_c.reshape(N_REP, N_EXP * CAP, D).astype(jnp.float32)
        rep_gate = grad_gate.reshape(N_REP, N_EXP * CAP, FF).astype(jnp.float32)
        rep_up = grad_up.reshape(N_REP, N_EXP * CAP, FF).astype(jnp.float32)
        rep_hidden = hidden.reshape(N_REP, N_EXP * CAP, FF).astype(jnp.float32)
        part_gate = jnp.einsum('rmd,rmf->rdf', rep_x, rep_gate).astype(jnp.bfloat16)
        part_up = jnp.einsum('rmd,rmf->rdf', rep_x, rep_up).astype(jnp.bfloat16)
        part_down = jnp.einsum('rmf,rmd->rfd', rep_hidden, rep_c).astype(jnp.bfloat16)
        total_gate = (jnp.sum(part_gate.astype(jnp.float32), axis=0) / N_REP).astype(jnp.bfloat16)
        total_up = (jnp.sum(part_up.astype(jnp.float32), axis=0) / N_REP).astype(jnp.bfloat16)
        total_down = (jnp.sum(part_down.astype(jnp.float32), axis=0) / N_REP).astype(jnp.bfloat16)
        target_token = (index // TOP).astype(jnp.int32)
        slot_weight = jnp.take_along_axis(weight_pairs, index, axis=1)
        out_acc = out_acc.at[device_rows, target_token].add(
            slot_weight[:, :, None] * output.reshape(devices_all, CAP, D).astype(jnp.float32))
        grad_acc = grad_acc.at[device_rows, target_token].add(
            grad_rows.reshape(devices_all, CAP, D).astype(jnp.float32))
        return (out_acc, grad_acc), (total_gate, total_up, total_down)

    start = (jnp.zeros((devices_all, TOK_DEV + 1, D), jnp.float32), jnp.zeros((devices_all, TOK_DEV + 1, D), jnp.float32))
    (out_acc, grad_acc), (gate_grad, up_grad, down_grad) = lax.scan(
        per_expert, start, jnp.arange(EXPERTS, dtype=jnp.int32))
    mixed = out_acc[:, :TOK_DEV].reshape(TOKENS, D).astype(jnp.bfloat16)
    token_grad = grad_acc[:, :TOK_DEV].reshape(TOKENS, D).astype(jnp.bfloat16)
    return (mixed, token_grad, gate_grad, up_grad, down_grad)
```

```python
import jax
import jax.numpy as jnp
from jax import lax
from jax.experimental import pallas as pl
from jax.experimental.pallas import tpu as pltpu
from jax.sharding import PartitionSpec as P

F32 = jnp.float32
BF16 = jnp.bfloat16
VMEM_BYTES = 50 * 1024 * 1024


def nn(a, b):
    return lax.dot_general(a, b, (((1,), (0,)), ((), ())), preferred_element_type=F32)


def nt(a, b):
    return lax.dot_general(a, b, (((1,), (1,)), ((), ())), preferred_element_type=F32)


def tn(a, b):
    return lax.dot_general(a, b, (((0,), (0,)), ((), ())), preferred_element_type=F32)


def call(body, out_shape, name, **kw):
    return pl.pallas_call(
        body,
        out_shape=out_shape,
        name=name,
        compiler_params=pltpu.CompilerParams(vmem_limit_bytes=VMEM_BYTES),
        **kw,
    )


def pack_weights(gate_ref, up_ref, down_ref, out_ref):
    out_ref[0] = gate_ref[...]
    out_ref[1] = up_ref[...]
    out_ref[2] = down_ref[...].T


def slot_onehots(ids_ref, experts, capacity):
    top, rows = ids_ref.shape
    expert = lax.broadcasted_iota(jnp.int32, (experts, rows), 0)
    hot = [(ids_ref[k : k + 1, :] == expert).astype(F32) for k in range(top)]
    earlier = lax.broadcasted_iota(jnp.int32, (rows, rows), 0) < lax.broadcasted_iota(
        jnp.int32, (rows, rows), 1
    )
    before = nn(sum(hot).astype(BF16), earlier.astype(BF16))
    place = lax.broadcasted_iota(jnp.int32, (experts * capacity, rows), 0)
    picks = []
    for k in range(top):
        slot = jnp.sum(before * hot[k], axis=0, keepdims=True).astype(jnp.int32)
        picks.append(place == ids_ref[k : k + 1, :] * capacity + slot)
    return picks


def dispatch(experts, capacity):
    def body(ids_ref, cw_ref, tok_ref, cot_ref, out_ref):
        picks = slot_onehots(ids_ref, experts, capacity)
        row_weight = sum(
            jnp.sum(jnp.where(p, cw_ref[k : k + 1, :], 0.0), axis=1, keepdims=True)
            for k, p in enumerate(picks)
        )
        pick = (picks[0] | picks[1]).astype(BF16)
        features = tok_ref.shape[1]
        out_ref[:, 0] = nn(pick, tok_ref[...]).astype(BF16).reshape(experts, capacity, features)
        weighted = (nn(pick, cot_ref[...]) * row_weight).astype(BF16)
        out_ref[:, 1] = weighted.reshape(experts, capacity, features)

    return body


def expert_grads(xc_ref, w_ref, grads_ref, hidden_ref, dg_ref, du_ref):
    groups, _, capacity, features = xc_ref.shape
    reps, _, part, ff = w_ref.shape
    rows = groups * capacity
    x = xc_ref[:, 0].reshape(rows, features)
    c = xc_ref[:, 1].reshape(rows, features)
    gate = nn(x, w_ref[:, 0].reshape(features, ff))
    up = nn(x, w_ref[:, 1].reshape(features, ff))
    dh = nn(c, w_ref[:, 2].reshape(features, ff))
    sigma = jax.nn.sigmoid(gate)
    swish = gate * sigma
    hidden_ref[...] = (swish * up).astype(BF16)
    dg_ref[...] = (dh * up * sigma * (1.0 + gate * (1.0 - sigma))).astype(BF16)
    du_ref[...] = (dh * swish).astype(BF16)
    grads_ref[:, 0] = tn(x, dg_ref[...]).astype(BF16).reshape(reps, part, ff)
    grads_ref[:, 1] = tn(x, du_ref[...]).astype(BF16).reshape(reps, part, ff)
    grads_ref[:, 2] = tn(c, hidden_ref[...]).astype(BF16).reshape(reps, part, ff)


def expert_rows(w_ref, hidden_ref, dg_ref, du_ref, out_ref):
    groups, _, capacity, features = out_ref.shape
    ff = w_ref.shape[3]
    dx = nt(dg_ref[...], w_ref[:, 0].reshape(features, ff)) + nt(
        du_ref[...], w_ref[:, 1].reshape(features, ff)
    )
    out_ref[:, 1] = dx.astype(BF16).reshape(groups, capacity, features)
    o = nt(hidden_ref[...], w_ref[:, 2].reshape(features, ff))
    out_ref[:, 0] = o.astype(BF16).reshape(groups, capacity, features)


def combine(ids_ref, cw_ref, back_ref, mixed_ref, grad_ref):
    experts, _, capacity, features = back_ref.shape
    top, rows = ids_ref.shape
    picks = [p.astype(BF16) for p in slot_onehots(ids_ref, experts, capacity)]
    o = back_ref[:, 0].reshape(experts * capacity, features)
    dx = back_ref[:, 1].reshape(experts * capacity, features)
    column = jnp.concatenate([cw_ref[...], jnp.zeros((8 - top, rows), F32)], axis=0).T
    mixed = sum(column[:, k : k + 1] * tn(p, o) for k, p in enumerate(picks))
    mixed_ref[...] = mixed.astype(BF16)
    grad_ref[...] = tn(picks[0] + picks[1], dx).astype(BF16)


def finish_grads(replicas):
    def body(red_ref, gate_ref, up_ref, down_ref):
        gate_ref[...] = (red_ref[0].astype(F32) / replicas).astype(BF16)
        up_ref[...] = (red_ref[1].astype(F32) / replicas).astype(BF16)
        down_ref[...] = (red_ref[2].astype(F32) / replicas).astype(BF16).T

    return body


def per_device(tokens, cotangent, expert_ids, combine_weight, gate_weight, up_weight, down_weight):
    tok_rows, features = tokens.shape
    groups = lax.axis_size("exp")
    replicas = lax.axis_size("rep")
    _, part, ff = gate_weight.shape
    capacity = 2 * tok_rows * expert_ids.shape[1] // groups
    rows = groups * capacity
    ids, cw = expert_ids.T, combine_weight.T
    sds = jax.ShapeDtypeStruct

    packed = call(pack_weights, sds((3, part, ff), BF16), "pack_weights")(
        gate_weight[0], up_weight[0], down_weight[0]
    )
    weights = lax.all_gather(packed, "rep", axis=0)
    wire = (groups, 2, capacity, features)
    sent = call(dispatch(groups, capacity), sds(wire, BF16), "dispatch")(
        ids, cw, tokens, cotangent
    )
    received = lax.all_to_all(sent, "exp", split_axis=0, concat_axis=0, tiled=True)
    grads, hidden, dg, du = call(
        expert_grads,
        (sds((replicas, 3, part, ff), BF16),) + (sds((rows, ff), BF16),) * 3,
        "expert_grads",
    )(received, weights)
    reduced = lax.psum_scatter(grads, "rep", scatter_dimension=0)
    results = call(expert_rows, sds(wire, BF16), "expert_rows")(weights, hidden, dg, du)
    back = lax.all_to_all(results, "exp", split_axis=0, concat_axis=0, tiled=True)
    mixed, token_grad = call(combine, (sds((tok_rows, features), BF16),) * 2, "combine")(
        ids, cw, back
    )
    gate_grad, up_grad, down_grad = call(
        finish_grads(replicas),
        (sds((part, ff), BF16), sds((part, ff), BF16), sds((ff, part), BF16)),
        "finish_grads",
    )(reduced)
    return (mixed, token_grad, gate_grad[None], up_grad[None], down_grad[None])


def solution(mesh):
    placed = (
        P(("rep", "exp"), None),
        P(("rep", "exp"), None),
        P(("rep", "exp"), None),
        P(("rep", "exp"), None),
        P("exp", "rep", None),
        P("exp", "rep", None),
        P("exp", None, "rep"),
    )
    return jax.shard_map(
        per_device,
        mesh=mesh,
        in_specs=placed,
        out_specs=(
            P(("rep", "exp"), None),
            P(("rep", "exp"), None),
            P("exp", "rep", None),
            P("exp", "rep", None),
            P("exp", None, "rep"),
        ),
        check_vma=False,
    )
```

```python
import jax
import jax.numpy as jnp
from jax import lax
from jax.experimental import pallas as pl
from jax.experimental.pallas import tpu as pltpu
from jax.sharding import PartitionSpec as P

F32 = jnp.float32
BF16 = jnp.bfloat16
VMEM_BYTES = 50 * 1024 * 1024


def nn(a, b):
    return lax.dot_general(a, b, (((1,), (0,)), ((), ())), preferred_element_type=F32)


def nt(a, b):
    return lax.dot_general(a, b, (((1,), (1,)), ((), ())), preferred_element_type=F32)


def tn(a, b):
    return lax.dot_general(a, b, (((0,), (0,)), ((), ())), preferred_element_type=F32)


HBM = pl.BlockSpec(memory_space=pltpu.HBM)
VMEM = pl.BlockSpec(memory_space=pltpu.VMEM)
copy = pltpu.make_async_copy


def call(body, out_shape, name, **kw):
    return pl.pallas_call(
        body,
        out_shape=out_shape,
        name=name,
        compiler_params=pltpu.CompilerParams(vmem_limit_bytes=VMEM_BYTES),
        **kw,
    )


def in_hbm(*arrays):
    return [pltpu.with_memory_space_constraint(a, pltpu.HBM) for a in arrays]


def run(copies):
    for c in copies:
        c.start()
    return copies


def drain(copies):
    for c in copies:
        c.wait()


def pack_weights(gate_hbm, up_hbm, down_hbm, out_hbm, down, turned, sems):
    fetch = copy(down_hbm, down, sems.at[0])
    fetch.start()
    rest = run([copy(gate_hbm, out_hbm.at[0], sems.at[1]), copy(up_hbm, out_hbm.at[1], sems.at[2])])
    fetch.wait()
    turned[...] = down[...].T
    rest += run([copy(turned, out_hbm.at[2], sems.at[3])])
    drain(rest)


def slot_onehots(ids_ref, experts, capacity):
    top, rows = ids_ref.shape
    expert = lax.broadcasted_iota(jnp.int32, (experts, rows), 0)
    hot = [(ids_ref[k : k + 1, :] == expert).astype(F32) for k in range(top)]
    earlier = lax.broadcasted_iota(jnp.int32, (rows, rows), 0) < lax.broadcasted_iota(
        jnp.int32, (rows, rows), 1
    )
    before = nn(sum(hot).astype(BF16), earlier.astype(BF16))
    place = lax.broadcasted_iota(jnp.int32, (experts * capacity, rows), 0)
    picks = []
    for k in range(top):
        slot = jnp.sum(before * hot[k], axis=0, keepdims=True).astype(jnp.int32)
        picks.append(place == ids_ref[k : k + 1, :] * capacity + slot)
    return picks


def dispatch(experts, capacity):
    def body(ids_hbm, cw_hbm, tok_hbm, cot_hbm, out_ref, ids_ref, cw_ref, tok, cot, sems):
        small = run([copy(ids_hbm, ids_ref, sems.at[2]), copy(cw_hbm, cw_ref, sems.at[3])])
        fetch = run([copy(tok_hbm, tok, sems.at[0]), copy(cot_hbm, cot, sems.at[1])])
        drain(small)
        picks = slot_onehots(ids_ref, experts, capacity)
        row_weight = sum(
            jnp.sum(jnp.where(p, cw_ref[k : k + 1, :], 0.0), axis=1, keepdims=True)
            for k, p in enumerate(picks)
        )
        pick = (picks[0] | picks[1]).astype(BF16)
        features = tok.shape[1]
        fetch[0].wait()
        out_ref[:, 0] = nn(pick, tok[...]).astype(BF16).reshape(experts, capacity, features)
        fetch[1].wait()
        weighted = (nn(pick, cot[...]) * row_weight).astype(BF16)
        out_ref[:, 1] = weighted.reshape(experts, capacity, features)

    return body


def experts_step(
    xc_ref, w_hbm, grads_hbm, out_hbm, w, g, out, hidden, dg, du, in_sems, grad_sems, out_sems
):
    groups, _, capacity, features = xc_ref.shape
    reps, _, part, ff = w_hbm.shape
    rows = groups * capacity
    fetch = run([copy(w_hbm.at[:, i], w.at[i], in_sems.at[i]) for i in range(3)])
    weight = lambda i: w[i].reshape(features, ff)
    x = lambda: xc_ref[:, 0].reshape(rows, features)
    c = lambda: xc_ref[:, 1].reshape(rows, features)
    fetch[0].wait()
    gate = nn(x(), weight(0))
    fetch[1].wait()
    up = nn(x(), weight(1))
    fetch[2].wait()
    dh = nn(c(), weight(2))
    sigma = jax.nn.sigmoid(gate)
    swish = gate * sigma
    hidden[...] = (swish * up).astype(BF16)
    dg[...] = (dh * up * sigma * (1.0 + gate * (1.0 - sigma))).astype(BF16)
    du[...] = (dh * swish).astype(BF16)
    pending = []
    half = reps // 2
    for i, (left, right) in enumerate(((x, dg), (x, du), (c, hidden))):
        for h in range(2):
            block = slice(h * half, (h + 1) * half)
            cols = slice(h * half * part, (h + 1) * half * part)
            g[i, block] = tn(left()[:, cols], right[...]).astype(BF16).reshape(half, part, ff)
            pending += run([copy(g.at[i, block], grads_hbm.at[block, i], grad_sems.at[i, h])])
    half = groups // 2
    for h in range(2):
        block = slice(h * half, (h + 1) * half)
        some = slice(h * half * capacity, (h + 1) * half * capacity)
        dx = nt(dg[some], weight(0)) + nt(du[some], weight(1))
        out[block, 1] = dx.astype(BF16).reshape(half, capacity, features)
        pending += run([copy(out.at[block, 1], out_hbm.at[block, 1], out_sems.at[1, h])])
        o = nt(hidden[some], weight(2))
        out[block, 0] = o.astype(BF16).reshape(half, capacity, features)
        pending += run([copy(out.at[block, 0], out_hbm.at[block, 0], out_sems.at[0, h])])
    drain(pending)


def finish(replicas):
    def body(
        ids_ref, cw_ref, back_ref, red_hbm, mixed_ref, grad_ref, gate_ref, up_ref, down_ref, red, sems
    ):
        fetch = run([copy(red_hbm, red, sems.at[0])])
        experts, _, capacity, features = back_ref.shape
        top, rows = ids_ref.shape
        picks = [p.astype(BF16) for p in slot_onehots(ids_ref, experts, capacity)]
        o = back_ref[:, 0].reshape(experts * capacity, features)
        dx = back_ref[:, 1].reshape(experts * capacity, features)
        column = jnp.concatenate([cw_ref[...], jnp.zeros((8 - top, rows), F32)], axis=0).T
        mixed = sum(column[:, k : k + 1] * tn(p, o) for k, p in enumerate(picks))
        mixed_ref[...] = mixed.astype(BF16)
        grad_ref[...] = tn(picks[0] + picks[1], dx).astype(BF16)
        drain(fetch)
        gate_ref[...] = (red[0].astype(F32) / replicas).astype(BF16)
        up_ref[...] = (red[1].astype(F32) / replicas).astype(BF16)
        down_ref[...] = (red[2].astype(F32) / replicas).astype(BF16).T

    return body


def per_device(tokens, cotangent, expert_ids, combine_weight, gate_weight, up_weight, down_weight):
    tok_rows, features = tokens.shape
    groups = lax.axis_size("exp")
    replicas = lax.axis_size("rep")
    _, part, ff = gate_weight.shape
    capacity = 2 * tok_rows * expert_ids.shape[1] // groups
    rows = groups * capacity
    ids, cw = expert_ids.T, combine_weight.T
    sds = jax.ShapeDtypeStruct

    sems = pltpu.SemaphoreType.DMA
    scratch = pltpu.VMEM
    packed = call(
        pack_weights,
        pltpu.HBM((3, part, ff), BF16),
        "pack_weights",
        in_specs=[HBM] * 3,
        out_specs=HBM,
        scratch_shapes=[scratch((ff, part), BF16), scratch((part, ff), BF16), sems((4,))],
    )(*in_hbm(gate_weight[0], up_weight[0], down_weight[0]))
    weights = lax.all_gather(packed, "rep", axis=0)
    wire = (groups, 2, capacity, features)
    sent = call(
        dispatch(groups, capacity),
        sds(wire, BF16),
        "dispatch",
        in_specs=[HBM] * 4,
        out_specs=VMEM,
        scratch_shapes=[scratch(ids.shape, jnp.int32), scratch(cw.shape, F32)]
        + [scratch(tokens.shape, BF16)] * 2
        + [sems((4,))],
    )(*in_hbm(ids, cw, tokens, cotangent))
    received = lax.all_to_all(sent, "exp", split_axis=0, concat_axis=0, tiled=True)
    grads, results = call(
        experts_step,
        (pltpu.HBM((replicas, 3, part, ff), BF16), pltpu.HBM(wire, BF16)),
        "experts_step",
        in_specs=[VMEM, HBM],
        out_specs=(HBM, HBM),
        scratch_shapes=[
            scratch((3, replicas, part, ff), BF16),
            scratch((3, replicas, part, ff), BF16),
            scratch(wire, BF16),
        ]
        + [scratch((rows, ff), BF16)] * 3
        + [sems((3,)), sems((3, 2)), sems((2, 2))],
    )(received, *in_hbm(weights))
    reduced = lax.psum_scatter(grads, "rep", scatter_dimension=0)
    back = lax.all_to_all(results, "exp", split_axis=0, concat_axis=0, tiled=True)
    mixed, token_grad, gate_grad, up_grad, down_grad = call(
        finish(replicas),
        (sds((tok_rows, features), BF16),) * 2
        + (sds((part, ff), BF16), sds((part, ff), BF16), sds((ff, part), BF16)),
        "finish",
        in_specs=[VMEM, VMEM, VMEM, HBM],
        out_specs=(VMEM,) * 5,
        scratch_shapes=[scratch((3, part, ff), BF16), sems((1,))],
    )(ids, cw, back, *in_hbm(reduced))
    return (mixed, token_grad, gate_grad[None], up_grad[None], down_grad[None])


def solution(mesh):
    placed = (
        P(("rep", "exp"), None),
        P(("rep", "exp"), None),
        P(("rep", "exp"), None),
        P(("rep", "exp"), None),
        P("exp", "rep", None),
        P("exp", "rep", None),
        P("exp", None, "rep"),
    )
    return jax.shard_map(
        per_device,
        mesh=mesh,
        in_specs=placed,
        out_specs=(
            P(("rep", "exp"), None),
            P(("rep", "exp"), None),
            P("exp", "rep", None),
            P("exp", "rep", None),
            P("exp", None, "rep"),
        ),
        check_vma=False,
    )
```

```python
import jax
import jax.numpy as jnp
from jax import lax
from jax.experimental import pallas as pl
from jax.experimental.pallas import tpu as pltpu
from jax.sharding import PartitionSpec as P

F32 = jnp.float32
BF16 = jnp.bfloat16
VMEM_BYTES = 50 * 1024 * 1024


def nn(a, b):
    return lax.dot_general(a, b, (((1,), (0,)), ((), ())), preferred_element_type=F32)


def nt(a, b):
    return lax.dot_general(a, b, (((1,), (1,)), ((), ())), preferred_element_type=F32)


def tn(a, b):
    return lax.dot_general(a, b, (((0,), (0,)), ((), ())), preferred_element_type=F32)


HBM = pl.BlockSpec(memory_space=pltpu.HBM)
VMEM = pl.BlockSpec(memory_space=pltpu.VMEM)
copy = pltpu.make_async_copy


def call(body, out_shape, name, **kw):
    return pl.pallas_call(
        body,
        out_shape=out_shape,
        name=name,
        compiler_params=pltpu.CompilerParams(vmem_limit_bytes=VMEM_BYTES),
        **kw,
    )


def in_hbm(*arrays):
    return [pltpu.with_memory_space_constraint(a, pltpu.HBM) for a in arrays]


def run(copies):
    for c in copies:
        c.start()
    return copies


def drain(copies):
    for c in copies:
        c.wait()


def pack_weights(gate_hbm, up_hbm, down_hbm, out_hbm, flat, down, sems):
    fetch = run(
        [
            copy(down_hbm, down, sems.at[2]),
            copy(gate_hbm, flat.at[0], sems.at[0]),
            copy(up_hbm, flat.at[1], sems.at[1]),
        ]
    )
    fetch[0].wait()
    flat[2] = down[...].T
    store = run([copy(flat.at[2], out_hbm.at[2], sems.at[2])])
    for i in range(2):
        fetch[i + 1].wait()
        store += run([copy(flat.at[i], out_hbm.at[i], sems.at[i])])
    drain(store)


def slot_onehots(ids_ref, experts, capacity):
    top, rows = ids_ref.shape
    expert = lax.broadcasted_iota(jnp.int32, (experts, rows), 0)
    hot = [(ids_ref[k : k + 1, :] == expert).astype(F32) for k in range(top)]
    earlier = lax.broadcasted_iota(jnp.int32, (rows, rows), 0) < lax.broadcasted_iota(
        jnp.int32, (rows, rows), 1
    )
    before = nn(sum(hot).astype(BF16), earlier.astype(BF16))
    place = lax.broadcasted_iota(jnp.int32, (experts * capacity, rows), 0)
    picks = []
    for k in range(top):
        slot = jnp.sum(before * hot[k], axis=0, keepdims=True).astype(jnp.int32)
        picks.append(place == ids_ref[k : k + 1, :] * capacity + slot)
    return picks


def dispatch(experts, capacity):
    def body(ids_hbm, cw_hbm, tok_hbm, cot_hbm, out_ref, ids_ref, cw_ref, tok, cot, sems):
        small = run([copy(ids_hbm, ids_ref, sems.at[2]), copy(cw_hbm, cw_ref, sems.at[3])])
        fetch = run([copy(tok_hbm, tok, sems.at[0]), copy(cot_hbm, cot, sems.at[1])])
        drain(small)
        picks = slot_onehots(ids_ref, experts, capacity)
        row_weight = sum(
            jnp.sum(jnp.where(p, cw_ref[k : k + 1, :], 0.0), axis=1, keepdims=True)
            for k, p in enumerate(picks)
        )
        pick = (picks[0] | picks[1]).astype(BF16)
        features = tok.shape[1]
        fetch[0].wait()
        out_ref[:, 0] = nn(pick, tok[...]).astype(BF16).reshape(experts, capacity, features)
        fetch[1].wait()
        weighted = (nn(pick, cot[...]) * row_weight).astype(BF16)
        out_ref[:, 1] = weighted.reshape(experts, capacity, features)

    return body


def experts_step(
    xc_ref, w_hbm, grads_hbm, out_hbm, w, g, out, hidden, dg, du, in_sems, grad_sems, out_sems
):
    groups, _, capacity, features = xc_ref.shape
    reps, _, part, ff = w_hbm.shape
    rows = groups * capacity
    fetch = run([copy(w_hbm.at[:, i], w.at[i], in_sems.at[i]) for i in range(3)])
    weight = lambda i: w[i].reshape(features, ff)
    x = lambda: xc_ref[:, 0].reshape(rows, features)
    c = lambda: xc_ref[:, 1].reshape(rows, features)
    fetch[0].wait()
    gate = nn(x(), weight(0))
    fetch[1].wait()
    up = nn(x(), weight(1))
    fetch[2].wait()
    dh = nn(c(), weight(2))
    sigma = jax.nn.sigmoid(gate)
    swish = gate * sigma
    hidden[...] = (swish * up).astype(BF16)
    dg[...] = (dh * up * sigma * (1.0 + gate * (1.0 - sigma))).astype(BF16)
    du[...] = (dh * swish).astype(BF16)
    pending = []
    half = reps // 2
    for i, (left, right) in enumerate(((x, dg), (x, du), (c, hidden))):
        for h in range(2):
            block = slice(h * half, (h + 1) * half)
            cols = slice(h * half * part, (h + 1) * half * part)
            g[i, block] = tn(left()[:, cols], right[...]).astype(BF16).reshape(half, part, ff)
            pending += run([copy(g.at[i, block], grads_hbm.at[block, i], grad_sems.at[i, h])])
    half = groups // 2
    for h in range(2):
        block = slice(h * half, (h + 1) * half)
        some = slice(h * half * capacity, (h + 1) * half * capacity)
        dx = nt(dg[some], weight(0)) + nt(du[some], weight(1))
        out[block, 1] = dx.astype(BF16).reshape(half, capacity, features)
        pending += run([copy(out.at[block, 1], out_hbm.at[block, 1], out_sems.at[1, h])])
        o = nt(hidden[some], weight(2))
        out[block, 0] = o.astype(BF16).reshape(half, capacity, features)
        pending += run([copy(out.at[block, 0], out_hbm.at[block, 0], out_sems.at[0, h])])
    drain(pending)


def finish(replicas):
    def body(ids_ref, cw_ref, back_ref, red_hbm, *rest):
        outs, (red, mixed, grad, scaled, turned, in_sems, out_sems) = rest[:5], rest[5:]
        mixed_hbm, grad_hbm, gate_hbm, up_hbm, down_hbm = outs
        fetch = run([copy(red_hbm.at[i], red.at[i], in_sems.at[i]) for i in range(3)])
        experts, _, capacity, features = back_ref.shape
        top, rows = ids_ref.shape
        picks = [p.astype(BF16) for p in slot_onehots(ids_ref, experts, capacity)]
        pending = []

        def store(value, index, source, target):
            source[...] = value
            pending.extend(run([copy(source, target, out_sems.at[index])]))

        dx = back_ref[:, 1].reshape(experts * capacity, features)
        store(tn(picks[0] + picks[1], dx).astype(BF16), 1, grad, grad_hbm)
        drain(fetch)
        store((red[2].astype(F32) / replicas).astype(BF16).T, 4, turned, down_hbm)
        store((red[0].astype(F32) / replicas).astype(BF16), 2, scaled.at[0], gate_hbm)
        store((red[1].astype(F32) / replicas).astype(BF16), 3, scaled.at[1], up_hbm)
        o = back_ref[:, 0].reshape(experts * capacity, features)
        column = jnp.concatenate([cw_ref[...], jnp.zeros((8 - top, rows), F32)], axis=0).T
        total = sum(column[:, k : k + 1] * tn(p, o) for k, p in enumerate(picks))
        store(total.astype(BF16), 0, mixed, mixed_hbm)
        drain(pending)

    return body


def per_device(tokens, cotangent, expert_ids, combine_weight, gate_weight, up_weight, down_weight):
    tok_rows, features = tokens.shape
    groups = lax.axis_size("exp")
    replicas = lax.axis_size("rep")
    _, part, ff = gate_weight.shape
    capacity = 2 * tok_rows * expert_ids.shape[1] // groups
    rows = groups * capacity
    ids, cw = expert_ids.T, combine_weight.T
    sds = jax.ShapeDtypeStruct

    sems = pltpu.SemaphoreType.DMA
    scratch = pltpu.VMEM
    packed = call(
        pack_weights,
        pltpu.HBM((3, part, ff), BF16),
        "pack_weights",
        in_specs=[HBM] * 3,
        out_specs=HBM,
        scratch_shapes=[scratch((3, part, ff), BF16), scratch((ff, part), BF16), sems((3,))],
    )(*in_hbm(gate_weight[0], up_weight[0], down_weight[0]))
    weights = lax.all_gather(packed, "rep", axis=0)
    wire = (groups, 2, capacity, features)
    sent = call(
        dispatch(groups, capacity),
        sds(wire, BF16),
        "dispatch",
        in_specs=[HBM] * 4,
        out_specs=VMEM,
        scratch_shapes=[scratch(ids.shape, jnp.int32), scratch(cw.shape, F32)]
        + [scratch(tokens.shape, BF16)] * 2
        + [sems((4,))],
    )(*in_hbm(ids, cw, tokens, cotangent))
    received = lax.all_to_all(sent, "exp", split_axis=0, concat_axis=0, tiled=True)
    grads, results = call(
        experts_step,
        (pltpu.HBM((replicas, 3, part, ff), BF16), pltpu.HBM(wire, BF16)),
        "experts_step",
        in_specs=[VMEM, HBM],
        out_specs=(HBM, HBM),
        scratch_shapes=[
            scratch((3, replicas, part, ff), BF16),
            scratch((3, replicas, part, ff), BF16),
            scratch(wire, BF16),
        ]
        + [scratch((rows, ff), BF16)] * 3
        + [sems((3,)), sems((3, 2)), sems((2, 2))],
    )(received, *in_hbm(weights))
    reduced = lax.psum_scatter(grads, "rep", scatter_dimension=0)
    back = lax.all_to_all(results, "exp", split_axis=0, concat_axis=0, tiled=True)
    mixed, token_grad, gate_grad, up_grad, down_grad = call(
        finish(replicas),
        (pltpu.HBM((tok_rows, features), BF16),) * 2
        + (pltpu.HBM((part, ff), BF16), pltpu.HBM((part, ff), BF16), pltpu.HBM((ff, part), BF16)),
        "finish",
        in_specs=[VMEM, VMEM, VMEM, HBM],
        out_specs=(HBM,) * 5,
        scratch_shapes=[scratch((3, part, ff), BF16)]
        + [scratch((tok_rows, features), BF16)] * 2
        + [scratch((2, part, ff), BF16), scratch((ff, part), BF16), sems((3,)), sems((5,))],
    )(ids, cw, back, *in_hbm(reduced))
    return (mixed, token_grad, gate_grad[None], up_grad[None], down_grad[None])


def solution(mesh):
    placed = (
        P(("rep", "exp"), None),
        P(("rep", "exp"), None),
        P(("rep", "exp"), None),
        P(("rep", "exp"), None),
        P("exp", "rep", None),
        P("exp", "rep", None),
        P("exp", None, "rep"),
    )
    return jax.shard_map(
        per_device,
        mesh=mesh,
        in_specs=placed,
        out_specs=(
            P(("rep", "exp"), None),
            P(("rep", "exp"), None),
            P("exp", "rep", None),
            P("exp", "rep", None),
            P("exp", None, "rep"),
        ),
        check_vma=False,
    )
```

```python
import jax
import jax.numpy as jnp
from jax import lax
from jax.experimental import pallas as pl
from jax.experimental.pallas import tpu as pltpu
from jax.sharding import PartitionSpec as P

F32 = jnp.float32
BF16 = jnp.bfloat16
VMEM_BYTES = 40 * 1024 * 1024


def nn(a, b):
    return lax.dot_general(a, b, (((1,), (0,)), ((), ())), preferred_element_type=F32)


def nt(a, b):
    return lax.dot_general(a, b, (((1,), (1,)), ((), ())), preferred_element_type=F32)


def tn(a, b):
    return lax.dot_general(a, b, (((0,), (0,)), ((), ())), preferred_element_type=F32)


HBM = pl.BlockSpec(memory_space=pltpu.HBM)
VMEM = pl.BlockSpec(memory_space=pltpu.VMEM)
copy = pltpu.make_async_copy


def call(body, out_shape, name, **kw):
    return pl.pallas_call(
        body,
        out_shape=out_shape,
        name=name,
        compiler_params=pltpu.CompilerParams(vmem_limit_bytes=VMEM_BYTES),
        **kw,
    )


def in_hbm(*arrays):
    return [pltpu.with_memory_space_constraint(a, pltpu.HBM) for a in arrays]


def run(copies):
    for c in copies:
        c.start()
    return copies


def drain(copies):
    for c in copies:
        c.wait()


def pack_weights(gate_hbm, up_hbm, down_hbm, out_hbm, flat, down, sems):
    fetch = run(
        [
            copy(down_hbm, down, sems.at[2]),
            copy(gate_hbm, flat.at[0], sems.at[0]),
            copy(up_hbm, flat.at[1], sems.at[1]),
        ]
    )
    fetch[0].wait()
    flat[2] = down[...].T
    store = run([copy(flat.at[2], out_hbm.at[2], sems.at[2])])
    for i in range(2):
        fetch[i + 1].wait()
        store += run([copy(flat.at[i], out_hbm.at[i], sems.at[i])])
    drain(store)


def slot_onehots(ids_ref, experts, capacity):
    top, rows = ids_ref.shape
    expert = lax.broadcasted_iota(jnp.int32, (experts, rows), 0)
    hot = [(ids_ref[k : k + 1, :] == expert).astype(F32) for k in range(top)]
    earlier = lax.broadcasted_iota(jnp.int32, (rows, rows), 0) < lax.broadcasted_iota(
        jnp.int32, (rows, rows), 1
    )
    before = nn(sum(hot).astype(BF16), earlier.astype(BF16))
    place = lax.broadcasted_iota(jnp.int32, (experts * capacity, rows), 0)
    picks = []
    for k in range(top):
        slot = jnp.sum(before * hot[k], axis=0, keepdims=True).astype(jnp.int32)
        picks.append(place == ids_ref[k : k + 1, :] * capacity + slot)
    return picks


def dispatch(experts, capacity):
    def body(ids_hbm, cw_hbm, tok_hbm, cot_hbm, out_ref, ids_ref, cw_ref, tok, cot, sems):
        small = run([copy(ids_hbm, ids_ref, sems.at[2]), copy(cw_hbm, cw_ref, sems.at[3])])
        fetch = run([copy(tok_hbm, tok, sems.at[0]), copy(cot_hbm, cot, sems.at[1])])
        drain(small)
        picks = slot_onehots(ids_ref, experts, capacity)
        row_weight = sum(
            jnp.sum(jnp.where(p, cw_ref[k : k + 1, :], 0.0), axis=1, keepdims=True)
            for k, p in enumerate(picks)
        )
        pick = (picks[0] | picks[1]).astype(BF16)
        features = tok.shape[1]
        fetch[0].wait()
        out_ref[:, 0] = nn(pick, tok[...]).astype(BF16).reshape(experts, capacity, features)
        fetch[1].wait()
        weighted = (nn(pick, cot[...]) * row_weight).astype(BF16)
        out_ref[:, 1] = weighted.reshape(experts, capacity, features)

    return body


def expert_grads(xc_ref, w_hbm, grads_hbm, mid_hbm, w, g, mid, in_sems, out_sems, mid_sems):
    hidden, dg, du = (mid.at[i] for i in range(3))
    groups, _, capacity, features = xc_ref.shape
    reps, _, part, ff = w_hbm.shape
    rows = groups * capacity
    fetch = run([copy(w_hbm.at[:, i], w.at[i], in_sems.at[i]) for i in range(3)])
    weight = lambda i: w[i].reshape(features, ff)
    x = lambda: xc_ref[:, 0].reshape(rows, features)
    c = lambda: xc_ref[:, 1].reshape(rows, features)
    pending = []
    half = reps // 2

    def keep(i, value):
        mid[i] = value.astype(BF16)
        pending.extend(run([copy(mid.at[i], mid_hbm.at[i], mid_sems.at[i])]))

    def store(i, left, right):
        for h in range(2):
            block = slice(h * half, (h + 1) * half)
            cols = slice(h * half * part, (h + 1) * half * part)
            g[i, block] = tn(left()[:, cols], right[...]).astype(BF16).reshape(half, part, ff)
            pending.extend(run([copy(g.at[i, block], grads_hbm.at[block, i], out_sems.at[i, h])]))

    fetch[0].wait()
    gate = nn(x(), weight(0))
    fetch[1].wait()
    up = nn(x(), weight(1))
    sigma = jax.nn.sigmoid(gate)
    swish = gate * sigma
    keep(0, swish * up)
    store(2, c, hidden)
    fetch[2].wait()
    dh = nn(c(), weight(2))
    keep(1, dh * up * sigma * (1.0 + gate * (1.0 - sigma)))
    keep(2, dh * swish)
    store(0, x, dg)
    store(1, x, du)
    drain(pending)


def expert_rows(w_hbm, mid_hbm, out_hbm, w, mid, out, in_sems, out_sems, mid_sems):
    hidden, dg, du = (mid.at[i] for i in range(3))
    groups, _, capacity, features = out_hbm.shape
    ff = w_hbm.shape[3]
    fetch = [copy(w_hbm.at[:, i], w.at[i], in_sems.at[i]) for i in range(3)]
    some = [copy(mid_hbm.at[i], mid.at[i], mid_sems.at[i]) for i in range(3)]
    run([some[0], fetch[2], some[1], some[2], fetch[0], fetch[1]])
    weight = lambda i: w[i].reshape(features, ff)
    pending = []
    half = groups // 2

    def store(k, h, value):
        block = slice(h * half, (h + 1) * half)
        out[block, k] = value.astype(BF16).reshape(half, capacity, features)
        pending.extend(run([copy(out.at[block, k], out_hbm.at[block, k], out_sems.at[k, h])]))

    span = [slice(h * half * capacity, (h + 1) * half * capacity) for h in range(2)]
    drain([some[0], fetch[2]])
    for h in range(2):
        store(0, h, nt(hidden[span[h]], weight(2)))
    drain(some[1:] + fetch[:2])
    for h in range(2):
        store(1, h, nt(dg[span[h]], weight(0)) + nt(du[span[h]], weight(1)))
    drain(pending)


def finish(replicas):
    def body(ids_ref, cw_ref, back_ref, red_hbm, *rest):
        outs, (red, mixed, grad, scaled, turned, in_sems, out_sems) = rest[:5], rest[5:]
        mixed_hbm, grad_hbm, gate_hbm, up_hbm, down_hbm = outs
        fetch = run([copy(red_hbm.at[i], red.at[i], in_sems.at[i]) for i in range(3)])
        experts, _, capacity, features = back_ref.shape
        top, rows = ids_ref.shape
        picks = [p.astype(BF16) for p in slot_onehots(ids_ref, experts, capacity)]
        pending = []

        def store(value, index, source, target):
            source[...] = value
            pending.extend(run([copy(source, target, out_sems.at[index])]))

        dx = back_ref[:, 1].reshape(experts * capacity, features)
        store(tn(picks[0] + picks[1], dx).astype(BF16), 1, grad, grad_hbm)
        drain(fetch)
        store((red[2].astype(F32) / replicas).astype(BF16).T, 4, turned, down_hbm)
        store((red[0].astype(F32) / replicas).astype(BF16), 2, scaled.at[0], gate_hbm)
        store((red[1].astype(F32) / replicas).astype(BF16), 3, scaled.at[1], up_hbm)
        o = back_ref[:, 0].reshape(experts * capacity, features)
        column = jnp.concatenate([cw_ref[...], jnp.zeros((8 - top, rows), F32)], axis=0).T
        total = sum(column[:, k : k + 1] * tn(p, o) for k, p in enumerate(picks))
        store(total.astype(BF16), 0, mixed, mixed_hbm)
        drain(pending)

    return body


def per_device(tokens, cotangent, expert_ids, combine_weight, gate_weight, up_weight, down_weight):
    tok_rows, features = tokens.shape
    groups = lax.axis_size("exp")
    replicas = lax.axis_size("rep")
    _, part, ff = gate_weight.shape
    capacity = 2 * tok_rows * expert_ids.shape[1] // groups
    rows = groups * capacity
    ids, cw = expert_ids.T, combine_weight.T
    sds = jax.ShapeDtypeStruct

    sems = pltpu.SemaphoreType.DMA
    scratch = pltpu.VMEM
    packed = call(
        pack_weights,
        pltpu.HBM((3, part, ff), BF16),
        "pack_weights",
        in_specs=[HBM] * 3,
        out_specs=HBM,
        scratch_shapes=[scratch((3, part, ff), BF16), scratch((ff, part), BF16), sems((3,))],
    )(*in_hbm(gate_weight[0], up_weight[0], down_weight[0]))
    weights = lax.all_gather(packed, "rep", axis=0)
    wire = (groups, 2, capacity, features)
    sent = call(
        dispatch(groups, capacity),
        sds(wire, BF16),
        "dispatch",
        in_specs=[HBM] * 4,
        out_specs=VMEM,
        scratch_shapes=[scratch(ids.shape, jnp.int32), scratch(cw.shape, F32)]
        + [scratch(tokens.shape, BF16)] * 2
        + [sems((4,))],
    )(*in_hbm(ids, cw, tokens, cotangent))
    received = lax.all_to_all(sent, "exp", split_axis=0, concat_axis=0, tiled=True)
    grads, mid = call(
        expert_grads,
        (pltpu.HBM((replicas, 3, part, ff), BF16), pltpu.HBM((3, rows, ff), BF16)),
        "expert_grads",
        in_specs=[VMEM, HBM],
        out_specs=(HBM, HBM),
        scratch_shapes=[scratch((3, replicas, part, ff), BF16)] * 2
        + [scratch((3, rows, ff), BF16), sems((3,)), sems((3, 2)), sems((3,))],
    )(received, *in_hbm(weights))
    reduced = lax.psum_scatter(grads, "rep", scatter_dimension=0)
    results = call(
        expert_rows,
        pltpu.HBM(wire, BF16),
        "expert_rows",
        in_specs=[HBM, HBM],
        out_specs=HBM,
        scratch_shapes=[
            scratch((3, replicas, part, ff), BF16),
            scratch((3, rows, ff), BF16),
            scratch(wire, BF16),
            sems((3,)),
            sems((2, 2)),
            sems((3,)),
        ],
    )(*in_hbm(weights, mid))
    back = lax.all_to_all(results, "exp", split_axis=0, concat_axis=0, tiled=True)
    mixed, token_grad, gate_grad, up_grad, down_grad = call(
        finish(replicas),
        (pltpu.HBM((tok_rows, features), BF16),) * 2
        + (pltpu.HBM((part, ff), BF16), pltpu.HBM((part, ff), BF16), pltpu.HBM((ff, part), BF16)),
        "finish",
        in_specs=[VMEM, VMEM, VMEM, HBM],
        out_specs=(HBM,) * 5,
        scratch_shapes=[scratch((3, part, ff), BF16)]
        + [scratch((tok_rows, features), BF16)] * 2
        + [scratch((2, part, ff), BF16), scratch((ff, part), BF16), sems((3,)), sems((5,))],
    )(ids, cw, back, *in_hbm(reduced))
    return (mixed, token_grad, gate_grad[None], up_grad[None], down_grad[None])


def solution(mesh):
    placed = (
        P(("rep", "exp"), None),
        P(("rep", "exp"), None),
        P(("rep", "exp"), None),
        P(("rep", "exp"), None),
        P("exp", "rep", None),
        P("exp", "rep", None),
        P("exp", None, "rep"),
    )
    return jax.shard_map(
        per_device,
        mesh=mesh,
        in_specs=placed,
        out_specs=(
            P(("rep", "exp"), None),
            P(("rep", "exp"), None),
            P("exp", "rep", None),
            P("exp", "rep", None),
            P("exp", None, "rep"),
        ),
        check_vma=False,
    )
```

```python
import jax
import jax.numpy as jnp
from jax import lax
from jax.experimental import pallas as pl
from jax.experimental.pallas import tpu as pltpu
from jax.sharding import PartitionSpec as P

F32 = jnp.float32
BF16 = jnp.bfloat16
VMEM_BYTES = 50 * 1024 * 1024


def nn(a, b):
    return lax.dot_general(a, b, (((1,), (0,)), ((), ())), preferred_element_type=F32)


def nt(a, b):
    return lax.dot_general(a, b, (((1,), (1,)), ((), ())), preferred_element_type=F32)


def tn(a, b):
    return lax.dot_general(a, b, (((0,), (0,)), ((), ())), preferred_element_type=F32)


HBM = pl.BlockSpec(memory_space=pltpu.HBM)
VMEM = pl.BlockSpec(memory_space=pltpu.VMEM)
copy = pltpu.make_async_copy


def call(body, out_shape, name, **kw):
    return pl.pallas_call(
        body,
        out_shape=out_shape,
        name=name,
        compiler_params=pltpu.CompilerParams(vmem_limit_bytes=VMEM_BYTES),
        **kw,
    )


def in_hbm(*arrays):
    return [pltpu.with_memory_space_constraint(a, pltpu.HBM) for a in arrays]


def run(copies):
    for c in copies:
        c.start()
    return copies


def drain(copies):
    for c in copies:
        c.wait()


def pack_weights(gate_hbm, up_hbm, down_hbm, out_hbm, flat, down, sems):
    fetch = run(
        [
            copy(down_hbm, down, sems.at[2]),
            copy(gate_hbm, flat.at[0], sems.at[0]),
            copy(up_hbm, flat.at[1], sems.at[1]),
        ]
    )
    fetch[0].wait()
    flat[2] = down[...].T
    store = run([copy(flat.at[2], out_hbm.at[2], sems.at[2])])
    for i in range(2):
        fetch[i + 1].wait()
        store += run([copy(flat.at[i], out_hbm.at[i], sems.at[i])])
    drain(store)


def slot_onehots(ids_ref, experts, capacity):
    top, rows = ids_ref.shape
    expert = lax.broadcasted_iota(jnp.int32, (experts, rows), 0)
    hot = [(ids_ref[k : k + 1, :] == expert).astype(F32) for k in range(top)]
    earlier = lax.broadcasted_iota(jnp.int32, (rows, rows), 0) < lax.broadcasted_iota(
        jnp.int32, (rows, rows), 1
    )
    before = nn(sum(hot).astype(BF16), earlier.astype(BF16))
    place = lax.broadcasted_iota(jnp.int32, (experts * capacity, rows), 0)
    spots = []
    for k in range(top):
        slot = jnp.sum(before * hot[k], axis=0, keepdims=True).astype(jnp.int32)
        spots.append(ids_ref[k : k + 1, :] * capacity + slot)
    return spots, [place == spot for spot in spots]


def dispatch(experts, capacity):
    def body(ids_hbm, cw_hbm, tok_hbm, cot_hbm, out_ref, table_ref, ids_ref, cw_ref, tok, cot, sems):
        small = run([copy(ids_hbm, ids_ref, sems.at[2]), copy(cw_hbm, cw_ref, sems.at[3])])
        fetch = run([copy(tok_hbm, tok, sems.at[0]), copy(cot_hbm, cot, sems.at[1])])
        drain(small)
        spots, picks = slot_onehots(ids_ref, experts, capacity)
        top, rows = ids_ref.shape
        lines = [spot.astype(F32) for spot in spots] + [cw_ref[...]]
        table_ref[...] = jnp.concatenate(lines + [jnp.zeros((8 - 2 * top, rows), F32)], axis=0).T
        row_weight = sum(
            jnp.sum(jnp.where(p, cw_ref[k : k + 1, :], 0.0), axis=1, keepdims=True)
            for k, p in enumerate(picks)
        )
        pick = (picks[0] | picks[1]).astype(BF16)
        features = tok.shape[1]
        fetch[0].wait()
        out_ref[:, 0] = nn(pick, tok[...]).astype(BF16).reshape(experts, capacity, features)
        fetch[1].wait()
        weighted = (nn(pick, cot[...]) * row_weight).astype(BF16)
        out_ref[:, 1] = weighted.reshape(experts, capacity, features)

    return body


def experts_step(
    xc_ref, w_hbm, grads_hbm, out_hbm, w, g, out, hidden, dg, du, in_sems, grad_sems, out_sems
):
    groups, _, capacity, features = xc_ref.shape
    reps, _, part, ff = w_hbm.shape
    rows = groups * capacity
    fetch = run([copy(w_hbm.at[:, i], w.at[i], in_sems.at[i]) for i in range(3)])
    weight = lambda i: w[i].reshape(features, ff)
    x = lambda: xc_ref[:, 0].reshape(rows, features)
    c = lambda: xc_ref[:, 1].reshape(rows, features)
    fetch[0].wait()
    gate = nn(x(), weight(0))
    fetch[1].wait()
    up = nn(x(), weight(1))
    fetch[2].wait()
    dh = nn(c(), weight(2))
    sigma = jax.nn.sigmoid(gate)
    swish = gate * sigma
    hidden[...] = (swish * up).astype(BF16)
    dg[...] = (dh * up * sigma * (1.0 + gate * (1.0 - sigma))).astype(BF16)
    du[...] = (dh * swish).astype(BF16)
    pending = []
    half = reps // 2
    for i, (left, right) in enumerate(((x, dg), (x, du), (c, hidden))):
        for h in range(2):
            block = slice(h * half, (h + 1) * half)
            cols = slice(h * half * part, (h + 1) * half * part)
            g[i, block] = tn(left()[:, cols], right[...]).astype(BF16).reshape(half, part, ff)
            pending += run([copy(g.at[i, block], grads_hbm.at[block, i], grad_sems.at[i, h])])
    half = groups // 2
    for h in range(2):
        block = slice(h * half, (h + 1) * half)
        some = slice(h * half * capacity, (h + 1) * half * capacity)
        dx = nt(dg[some], weight(0)) + nt(du[some], weight(1))
        out[block, 1] = dx.astype(BF16).reshape(half, capacity, features)
        pending += run([copy(out.at[block, 1], out_hbm.at[block, 1], out_sems.at[1, h])])
        o = nt(hidden[some], weight(2))
        out[block, 0] = o.astype(BF16).reshape(half, capacity, features)
        pending += run([copy(out.at[block, 0], out_hbm.at[block, 0], out_sems.at[0, h])])
    drain(pending)


def finish(replicas):
    def body(table_ref, back_ref, red_hbm, *rest):
        outs, (red, mixed, grad, scaled, turned, in_sems, out_sems) = rest[:5], rest[5:]
        mixed_hbm, grad_hbm, gate_hbm, up_hbm, down_hbm = outs
        fetch = run([copy(red_hbm.at[i], red.at[i], in_sems.at[i]) for i in range(3)])
        experts, _, capacity, features = back_ref.shape
        table = table_ref[...]
        place = lax.broadcasted_iota(jnp.int32, (table.shape[0], experts * capacity), 1)
        picks = [(place == table[:, k : k + 1].astype(jnp.int32)).astype(BF16) for k in range(2)]
        pending = []

        def store(value, index, source, target):
            source[...] = value
            pending.extend(run([copy(source, target, out_sems.at[index])]))

        dx = back_ref[:, 1].reshape(experts * capacity, features)
        store(nn(picks[0] + picks[1], dx).astype(BF16), 1, grad, grad_hbm)
        drain(fetch)
        store((red[2].astype(F32) / replicas).astype(BF16).T, 4, turned, down_hbm)
        store((red[0].astype(F32) / replicas).astype(BF16), 2, scaled.at[0], gate_hbm)
        store((red[1].astype(F32) / replicas).astype(BF16), 3, scaled.at[1], up_hbm)
        o = back_ref[:, 0].reshape(experts * capacity, features)
        total = sum(table[:, k + 2 : k + 3] * nn(p, o) for k, p in enumerate(picks))
        store(total.astype(BF16), 0, mixed, mixed_hbm)
        drain(pending)

    return body


def per_device(tokens, cotangent, expert_ids, combine_weight, gate_weight, up_weight, down_weight):
    tok_rows, features = tokens.shape
    groups = lax.axis_size("exp")
    replicas = lax.axis_size("rep")
    _, part, ff = gate_weight.shape
    capacity = 2 * tok_rows * expert_ids.shape[1] // groups
    rows = groups * capacity
    ids, cw = expert_ids.T, combine_weight.T
    sds = jax.ShapeDtypeStruct

    sems = pltpu.SemaphoreType.DMA
    scratch = pltpu.VMEM
    packed = call(
        pack_weights,
        pltpu.HBM((3, part, ff), BF16),
        "pack_weights",
        in_specs=[HBM] * 3,
        out_specs=HBM,
        scratch_shapes=[scratch((3, part, ff), BF16), scratch((ff, part), BF16), sems((3,))],
    )(*in_hbm(gate_weight[0], up_weight[0], down_weight[0]))
    weights = lax.all_gather(packed, "rep", axis=0)
    wire = (groups, 2, capacity, features)
    sent, table = call(
        dispatch(groups, capacity),
        (sds(wire, BF16), sds((tok_rows, 8), F32)),
        "dispatch",
        in_specs=[HBM] * 4,
        out_specs=(VMEM, VMEM),
        scratch_shapes=[scratch(ids.shape, jnp.int32), scratch(cw.shape, F32)]
        + [scratch(tokens.shape, BF16)] * 2
        + [sems((4,))],
    )(*in_hbm(ids, cw, tokens, cotangent))
    received = lax.all_to_all(sent, "exp", split_axis=0, concat_axis=0, tiled=True)
    grads, results = call(
        experts_step,
        (pltpu.HBM((replicas, 3, part, ff), BF16), pltpu.HBM(wire, BF16)),
        "experts_step",
        in_specs=[VMEM, HBM],
        out_specs=(HBM, HBM),
        scratch_shapes=[
            scratch((3, replicas, part, ff), BF16),
            scratch((3, replicas, part, ff), BF16),
            scratch(wire, BF16),
        ]
        + [scratch((rows, ff), BF16)] * 3
        + [sems((3,)), sems((3, 2)), sems((2, 2))],
    )(received, *in_hbm(weights))
    reduced = lax.psum_scatter(grads, "rep", scatter_dimension=0)
    back = lax.all_to_all(results, "exp", split_axis=0, concat_axis=0, tiled=True)
    mixed, token_grad, gate_grad, up_grad, down_grad = call(
        finish(replicas),
        (pltpu.HBM((tok_rows, features), BF16),) * 2
        + (pltpu.HBM((part, ff), BF16), pltpu.HBM((part, ff), BF16), pltpu.HBM((ff, part), BF16)),
        "finish",
        in_specs=[VMEM, VMEM, HBM],
        out_specs=(HBM,) * 5,
        scratch_shapes=[scratch((3, part, ff), BF16)]
        + [scratch((tok_rows, features), BF16)] * 2
        + [scratch((2, part, ff), BF16), scratch((ff, part), BF16), sems((3,)), sems((5,))],
    )(table, back, *in_hbm(reduced))
    return (mixed, token_grad, gate_grad[None], up_grad[None], down_grad[None])


def solution(mesh):
    placed = (
        P(("rep", "exp"), None),
        P(("rep", "exp"), None),
        P(("rep", "exp"), None),
        P(("rep", "exp"), None),
        P("exp", "rep", None),
        P("exp", "rep", None),
        P("exp", None, "rep"),
    )
    return jax.shard_map(
        per_device,
        mesh=mesh,
        in_specs=placed,
        out_specs=(
            P(("rep", "exp"), None),
            P(("rep", "exp"), None),
            P("exp", "rep", None),
            P("exp", "rep", None),
            P("exp", None, "rep"),
        ),
        check_vma=False,
    )
```

```python
import jax
import jax.numpy as jnp
from jax import lax
from jax.experimental import pallas as pl
from jax.experimental.pallas import tpu as pltpu
from jax.sharding import PartitionSpec as P

F32 = jnp.float32
BF16 = jnp.bfloat16
VMEM_BYTES = 50 * 1024 * 1024


def nn(a, b):
    return lax.dot_general(a, b, (((1,), (0,)), ((), ())), preferred_element_type=F32)


def nt(a, b):
    return lax.dot_general(a, b, (((1,), (1,)), ((), ())), preferred_element_type=F32)


def tn(a, b):
    return lax.dot_general(a, b, (((0,), (0,)), ((), ())), preferred_element_type=F32)


HBM = pl.BlockSpec(memory_space=pltpu.HBM)
VMEM = pl.BlockSpec(memory_space=pltpu.VMEM)
copy = pltpu.make_async_copy


def call(body, out_shape, name, **kw):
    return pl.pallas_call(
        body,
        out_shape=out_shape,
        name=name,
        compiler_params=pltpu.CompilerParams(vmem_limit_bytes=VMEM_BYTES),
        **kw,
    )


def in_hbm(*arrays):
    return [pltpu.with_memory_space_constraint(a, pltpu.HBM) for a in arrays]


def run(copies):
    for c in copies:
        c.start()
    return copies


def drain(copies):
    for c in copies:
        c.wait()


def pack_weights(gate_hbm, up_hbm, down_hbm, out_hbm, flat, down, sems):
    fetch = run(
        [
            copy(down_hbm, down, sems.at[2]),
            copy(gate_hbm, flat.at[0], sems.at[0]),
            copy(up_hbm, flat.at[1], sems.at[1]),
        ]
    )
    fetch[0].wait()
    flat[2] = down[...].T
    store = run([copy(flat.at[2], out_hbm.at[2], sems.at[2])])
    for i in range(2):
        fetch[i + 1].wait()
        store += run([copy(flat.at[i], out_hbm.at[i], sems.at[i])])
    drain(store)


def slot_onehots(ids_ref, experts, capacity):
    top, rows = ids_ref.shape
    expert = lax.broadcasted_iota(jnp.int32, (experts, rows), 0)
    hot = [(ids_ref[k : k + 1, :] == expert).astype(F32) for k in range(top)]
    earlier = lax.broadcasted_iota(jnp.int32, (rows, rows), 0) < lax.broadcasted_iota(
        jnp.int32, (rows, rows), 1
    )
    before = nn(sum(hot).astype(BF16), earlier.astype(BF16))
    place = lax.broadcasted_iota(jnp.int32, (experts * capacity, rows), 0)
    spots = []
    for k in range(top):
        slot = jnp.sum(before * hot[k], axis=0, keepdims=True).astype(jnp.int32)
        spots.append(ids_ref[k : k + 1, :] * capacity + slot)
    return spots, [place == spot for spot in spots]


def dispatch(experts, capacity):
    def body(ids_hbm, cw_hbm, tok_hbm, cot_hbm, out_ref, table_ref, ids_ref, cw_ref, tok, cot, sems):
        small = run([copy(ids_hbm, ids_ref, sems.at[2]), copy(cw_hbm, cw_ref, sems.at[3])])
        fetch = run([copy(tok_hbm, tok, sems.at[0]), copy(cot_hbm, cot, sems.at[1])])
        drain(small)
        spots, picks = slot_onehots(ids_ref, experts, capacity)
        top, rows = ids_ref.shape
        lines = [spot.astype(F32) for spot in spots] + [cw_ref[...]]
        table_ref[...] = jnp.concatenate(lines + [jnp.zeros((8 - 2 * top, rows), F32)], axis=0).T
        row_weight = sum(
            jnp.sum(jnp.where(p, cw_ref[k : k + 1, :], 0.0), axis=1, keepdims=True)
            for k, p in enumerate(picks)
        )
        pick = (picks[0] | picks[1]).astype(BF16)
        features = tok.shape[1]
        fetch[0].wait()
        out_ref[:, 0] = nn(pick, tok[...]).astype(BF16).reshape(experts, capacity, features)
        fetch[1].wait()
        weighted = (nn(pick, cot[...]) * row_weight).astype(BF16)
        out_ref[:, 1] = weighted.reshape(experts, capacity, features)

    return body


def experts_step(
    xc_ref, w_hbm, grads_hbm, out_hbm, w, g, out, hidden, dg, du, in_sems, grad_sems, out_sems
):
    groups, _, capacity, features = xc_ref.shape
    reps, _, part, ff = w_hbm.shape
    rows = groups * capacity
    fetch = run([copy(w_hbm.at[:, i], w.at[i], in_sems.at[i]) for i in range(3)])
    weight = lambda i: w[i].reshape(features, ff)
    x = lambda: xc_ref[:, 0].reshape(rows, features)
    c = lambda: xc_ref[:, 1].reshape(rows, features)
    fetch[0].wait()
    gate = nn(x(), weight(0))
    fetch[1].wait()
    up = nn(x(), weight(1))
    fetch[2].wait()
    dh = nn(c(), weight(2))
    sigma = jax.nn.sigmoid(gate)
    swish = gate * sigma
    hidden[...] = (swish * up).astype(BF16)
    dg[...] = (dh * up * sigma * (1.0 + gate * (1.0 - sigma))).astype(BF16)
    du[...] = (dh * swish).astype(BF16)
    pending = []
    half = reps // 2
    for i, (left, right) in enumerate(((x, dg), (x, du), (c, hidden))):
        for h in range(2):
            block = slice(h * half, (h + 1) * half)
            cols = slice(h * half * part, (h + 1) * half * part)
            g[i, block] = tn(left()[:, cols], right[...]).astype(BF16).reshape(half, part, ff)
            pending += run([copy(g.at[i, block], grads_hbm.at[block, i], grad_sems.at[i, h])])
    half = groups // 2
    for h in range(2):
        block = slice(h * half, (h + 1) * half)
        some = slice(h * half * capacity, (h + 1) * half * capacity)
        dx = nt(dg[some], weight(0)) + nt(du[some], weight(1))
        out[block, 1] = dx.astype(BF16).reshape(half, capacity, features)
        pending += run([copy(out.at[block, 1], out_hbm.at[block, 1], out_sems.at[1, h])])
        o = nt(hidden[some], weight(2))
        out[block, 0] = o.astype(BF16).reshape(half, capacity, features)
        pending += run([copy(out.at[block, 0], out_hbm.at[block, 0], out_sems.at[0, h])])
    drain(pending)


def finish(replicas):
    def body(table_ref, back_ref, red_hbm, *rest):
        outs, (red, mixed, grad, scaled, turned, in_sems, out_sems) = rest[:5], rest[5:]
        mixed_hbm, grad_hbm, gate_hbm, up_hbm, down_hbm = outs
        fetch = run([copy(red_hbm.at[i], red.at[i], in_sems.at[i]) for i in range(3)])
        experts, _, capacity, features = back_ref.shape
        table = table_ref[...]
        place = lax.broadcasted_iota(jnp.int32, (table.shape[0], experts * capacity), 1)
        picks = [(place == table[:, k : k + 1].astype(jnp.int32)).astype(BF16) for k in range(2)]
        pending = []

        def store(value, index, source, target):
            source[...] = value
            pending.extend(run([copy(source, target, out_sems.at[index])]))

        dx = back_ref[:, 1].reshape(experts * capacity, features)
        store(nn(picks[0] + picks[1], dx).astype(BF16), 1, grad, grad_hbm)
        drain(fetch)
        store((red[2].astype(F32) / replicas).astype(BF16).T, 4, turned, down_hbm)
        store((red[0].astype(F32) / replicas).astype(BF16), 2, scaled.at[0], gate_hbm)
        store((red[1].astype(F32) / replicas).astype(BF16), 3, scaled.at[1], up_hbm)
        o = back_ref[:, 0].reshape(experts * capacity, features)
        total = sum(table[:, k + 2 : k + 3] * nn(p, o) for k, p in enumerate(picks))
        store(total.astype(BF16), 0, mixed, mixed_hbm)
        drain(pending)

    return body


def per_device(tokens, cotangent, expert_ids, combine_weight, gate_weight, up_weight, down_weight):
    tok_rows, features = tokens.shape
    groups = lax.axis_size("exp")
    replicas = lax.axis_size("rep")
    _, part, ff = gate_weight.shape
    capacity = 2 * tok_rows * expert_ids.shape[1] // groups
    rows = groups * capacity
    ids, cw = expert_ids.T, combine_weight.T
    sds = jax.ShapeDtypeStruct

    sems = pltpu.SemaphoreType.DMA
    scratch = pltpu.VMEM
    packed = call(
        pack_weights,
        pltpu.HBM((3, part, ff), BF16),
        "pack_weights",
        in_specs=[HBM] * 3,
        out_specs=HBM,
        scratch_shapes=[scratch((3, part, ff), BF16), scratch((ff, part), BF16), sems((3,))],
    )(*in_hbm(gate_weight[0], up_weight[0], down_weight[0]))
    weights = lax.all_gather(packed.reshape(3 * part, ff), "rep", axis=0, tiled=True)
    weights = weights.reshape(replicas, 3, part, ff)
    wire = (groups, 2, capacity, features)
    sent, table = call(
        dispatch(groups, capacity),
        (sds(wire, BF16), sds((tok_rows, 8), F32)),
        "dispatch",
        in_specs=[HBM] * 4,
        out_specs=(VMEM, VMEM),
        scratch_shapes=[scratch(ids.shape, jnp.int32), scratch(cw.shape, F32)]
        + [scratch(tokens.shape, BF16)] * 2
        + [sems((4,))],
    )(*in_hbm(ids, cw, tokens, cotangent))
    received = lax.all_to_all(sent, "exp", split_axis=0, concat_axis=0, tiled=True)
    grads, results = call(
        experts_step,
        (pltpu.HBM((replicas, 3, part, ff), BF16), pltpu.HBM(wire, BF16)),
        "experts_step",
        in_specs=[VMEM, HBM],
        out_specs=(HBM, HBM),
        scratch_shapes=[
            scratch((3, replicas, part, ff), BF16),
            scratch((3, replicas, part, ff), BF16),
            scratch(wire, BF16),
        ]
        + [scratch((rows, ff), BF16)] * 3
        + [sems((3,)), sems((3, 2)), sems((2, 2))],
    )(received, *in_hbm(weights))
    grads = grads.reshape(replicas * 3 * part, ff)
    reduced = lax.psum_scatter(grads, "rep", scatter_dimension=0, tiled=True)
    reduced = reduced.reshape(3, part, ff)
    back = lax.all_to_all(results, "exp", split_axis=0, concat_axis=0, tiled=True)
    mixed, token_grad, gate_grad, up_grad, down_grad = call(
        finish(replicas),
        (pltpu.HBM((tok_rows, features), BF16),) * 2
        + (pltpu.HBM((part, ff), BF16), pltpu.HBM((part, ff), BF16), pltpu.HBM((ff, part), BF16)),
        "finish",
        in_specs=[VMEM, VMEM, HBM],
        out_specs=(HBM,) * 5,
        scratch_shapes=[scratch((3, part, ff), BF16)]
        + [scratch((tok_rows, features), BF16)] * 2
        + [scratch((2, part, ff), BF16), scratch((ff, part), BF16), sems((3,)), sems((5,))],
    )(table, back, *in_hbm(reduced))
    return (mixed, token_grad, gate_grad[None], up_grad[None], down_grad[None])


def solution(mesh):
    placed = (
        P(("rep", "exp"), None),
        P(("rep", "exp"), None),
        P(("rep", "exp"), None),
        P(("rep", "exp"), None),
        P("exp", "rep", None),
        P("exp", "rep", None),
        P("exp", None, "rep"),
    )
    return jax.shard_map(
        per_device,
        mesh=mesh,
        in_specs=placed,
        out_specs=(
            P(("rep", "exp"), None),
            P(("rep", "exp"), None),
            P("exp", "rep", None),
            P("exp", "rep", None),
            P("exp", None, "rep"),
        ),
        check_vma=False,
    )
```

```python
import jax
import jax.numpy as jnp
from jax import lax
from jax.experimental import pallas as pl
from jax.experimental.pallas import tpu as pltpu
from jax.sharding import PartitionSpec as P

F32 = jnp.float32
BF16 = jnp.bfloat16
VMEM_BYTES = 50 * 1024 * 1024


def nn(a, b):
    return lax.dot_general(a, b, (((1,), (0,)), ((), ())), preferred_element_type=F32)


def nt(a, b):
    return lax.dot_general(a, b, (((1,), (1,)), ((), ())), preferred_element_type=F32)


def tn(a, b):
    return lax.dot_general(a, b, (((0,), (0,)), ((), ())), preferred_element_type=F32)


HBM = pl.BlockSpec(memory_space=pltpu.HBM)
VMEM = pl.BlockSpec(memory_space=pltpu.VMEM)
copy = pltpu.make_async_copy


def call(body, out_shape, name, **kw):
    return pl.pallas_call(
        body,
        out_shape=out_shape,
        name=name,
        compiler_params=pltpu.CompilerParams(vmem_limit_bytes=VMEM_BYTES),
        **kw,
    )


def in_hbm(*arrays):
    return [pltpu.with_memory_space_constraint(a, pltpu.HBM) for a in arrays]


def run(copies):
    for c in copies:
        c.start()
    return copies


def drain(copies):
    for c in copies:
        c.wait()


def pack_weights(gate_hbm, up_hbm, down_hbm, out_hbm, flat, down, sems):
    fetch = run(
        [
            copy(down_hbm, down, sems.at[2]),
            copy(gate_hbm, flat.at[0], sems.at[0]),
            copy(up_hbm, flat.at[1], sems.at[1]),
        ]
    )
    fetch[0].wait()
    flat[2] = down[...].T
    store = run([copy(flat.at[2], out_hbm.at[2], sems.at[2])])
    for i in range(2):
        fetch[i + 1].wait()
        store += run([copy(flat.at[i], out_hbm.at[i], sems.at[i])])
    drain(store)


def slot_onehots(ids_ref, experts, capacity):
    top, rows = ids_ref.shape
    expert = lax.broadcasted_iota(jnp.int32, (experts, rows), 0)
    hot = [(ids_ref[k : k + 1, :] == expert).astype(F32) for k in range(top)]
    earlier = lax.broadcasted_iota(jnp.int32, (rows, rows), 0) < lax.broadcasted_iota(
        jnp.int32, (rows, rows), 1
    )
    before = nn(sum(hot).astype(BF16), earlier.astype(BF16))
    place = lax.broadcasted_iota(jnp.int32, (experts * capacity, rows), 0)
    spots = []
    for k in range(top):
        slot = jnp.sum(before * hot[k], axis=0, keepdims=True).astype(jnp.int32)
        spots.append(ids_ref[k : k + 1, :] * capacity + slot)
    return spots, [place == spot for spot in spots]


def dispatch(experts, capacity):
    def body(ids_hbm, cw_hbm, tok_hbm, cot_hbm, out_ref, table_ref, ids_ref, cw_ref, tok, cot, sems):
        small = run([copy(ids_hbm, ids_ref, sems.at[2]), copy(cw_hbm, cw_ref, sems.at[3])])
        fetch = run([copy(tok_hbm, tok, sems.at[0]), copy(cot_hbm, cot, sems.at[1])])
        drain(small)
        spots, picks = slot_onehots(ids_ref, experts, capacity)
        top, rows = ids_ref.shape
        lines = [spot.astype(F32) for spot in spots] + [cw_ref[...]]
        table_ref[...] = jnp.concatenate(lines + [jnp.zeros((8 - 2 * top, rows), F32)], axis=0).T
        row_weight = sum(
            jnp.sum(jnp.where(p, cw_ref[k : k + 1, :], 0.0), axis=1, keepdims=True)
            for k, p in enumerate(picks)
        )
        pick = (picks[0] | picks[1]).astype(BF16)
        features = tok.shape[1]
        fetch[0].wait()
        out_ref[:, 0] = nn(pick, tok[...]).astype(BF16).reshape(experts, capacity, features)
        fetch[1].wait()
        weighted = (nn(pick, cot[...]) * row_weight).astype(BF16)
        out_ref[:, 1] = weighted.reshape(experts, capacity, features)

    return body


def experts_step(
    xc_ref, w_hbm, grads_hbm, out_hbm, w, g, out, hidden, dg, du, in_sems, grad_sems, out_sems
):
    groups, _, capacity, features = xc_ref.shape
    reps, _, part, ff = w_hbm.shape
    rows = groups * capacity
    fetch = run([copy(w_hbm.at[:, i], w.at[i], in_sems.at[i]) for i in range(3)])
    weight = lambda i: w[i].reshape(features, ff)
    x = lambda: xc_ref[:, 0].reshape(rows, features)
    c = lambda: xc_ref[:, 1].reshape(rows, features)
    fetch[0].wait()
    gate = nn(x(), weight(0))
    fetch[1].wait()
    up = nn(x(), weight(1))
    fetch[2].wait()
    dh = nn(c(), weight(2))
    sigma = jax.nn.sigmoid(gate)
    swish = gate * sigma
    hidden[...] = (swish * up).astype(BF16)
    dg[...] = (dh * up * sigma * (1.0 + gate * (1.0 - sigma))).astype(BF16)
    du[...] = (dh * swish).astype(BF16)
    pending = []
    half = reps // 2
    for i, (left, right) in enumerate(((x, dg), (x, du), (c, hidden))):
        for h in range(2):
            block = slice(h * half, (h + 1) * half)
            cols = slice(h * half * part, (h + 1) * half * part)
            g[i, block] = tn(left()[:, cols], right[...]).astype(BF16).reshape(half, part, ff)
            pending += run([copy(g.at[i, block], grads_hbm.at[block, i], grad_sems.at[i, h])])
    half = groups // 2
    for h in range(2):
        block = slice(h * half, (h + 1) * half)
        some = slice(h * half * capacity, (h + 1) * half * capacity)
        dx = nt(dg[some], weight(0)) + nt(du[some], weight(1))
        out[block, 1] = dx.astype(BF16).reshape(half, capacity, features)
        pending += run([copy(out.at[block, 1], out_hbm.at[block, 1], out_sems.at[1, h])])
        o = nt(hidden[some], weight(2))
        out[block, 0] = o.astype(BF16).reshape(half, capacity, features)
        pending += run([copy(out.at[block, 0], out_hbm.at[block, 0], out_sems.at[0, h])])
    drain(pending)


def combine(table_ref, back_ref, mixed_hbm, grad_hbm, mixed, grad, sems):
    experts, _, capacity, features = back_ref.shape
    table = table_ref[...]
    place = lax.broadcasted_iota(jnp.int32, (table.shape[0], experts * capacity), 1)
    picks = [(place == table[:, k : k + 1].astype(jnp.int32)).astype(BF16) for k in range(2)]
    dx = back_ref[:, 1].reshape(experts * capacity, features)
    grad[...] = nn(picks[0] + picks[1], dx).astype(BF16)
    pending = run([copy(grad, grad_hbm, sems.at[1])])
    o = back_ref[:, 0].reshape(experts * capacity, features)
    total = sum(table[:, k + 2 : k + 3] * nn(p, o) for k, p in enumerate(picks))
    mixed[...] = total.astype(BF16)
    drain(pending + run([copy(mixed, mixed_hbm, sems.at[0])]))


def average_grads(replicas):
    def body(red_hbm, gate_hbm, up_hbm, down_hbm, red, scaled, turned, in_sems, out_sems):
        fetch = [copy(red_hbm.at[i], red.at[i], in_sems.at[i]) for i in range(3)]
        run([fetch[2], fetch[0], fetch[1]])
        mean = lambda i: (red[i].astype(F32) / replicas).astype(BF16)
        fetch[2].wait()
        turned[...] = mean(2).T
        pending = run([copy(turned, down_hbm, out_sems.at[2])])
        for i, target in enumerate((gate_hbm, up_hbm)):
            fetch[i].wait()
            scaled[i] = mean(i)
            pending += run([copy(scaled.at[i], target, out_sems.at[i])])
        drain(pending)

    return body


def per_device(tokens, cotangent, expert_ids, combine_weight, gate_weight, up_weight, down_weight):
    tok_rows, features = tokens.shape
    groups = lax.axis_size("exp")
    replicas = lax.axis_size("rep")
    _, part, ff = gate_weight.shape
    capacity = 2 * tok_rows * expert_ids.shape[1] // groups
    rows = groups * capacity
    ids, cw = expert_ids.T, combine_weight.T
    sds = jax.ShapeDtypeStruct

    sems = pltpu.SemaphoreType.DMA
    scratch = pltpu.VMEM
    packed = call(
        pack_weights,
        pltpu.HBM((3, part, ff), BF16),
        "pack_weights",
        in_specs=[HBM] * 3,
        out_specs=HBM,
        scratch_shapes=[scratch((3, part, ff), BF16), scratch((ff, part), BF16), sems((3,))],
    )(*in_hbm(gate_weight[0], up_weight[0], down_weight[0]))
    weights = lax.all_gather(packed.reshape(3 * part, ff), "rep", axis=0, tiled=True)
    weights = weights.reshape(replicas, 3, part, ff)
    wire = (groups, 2, capacity, features)
    sent, table = call(
        dispatch(groups, capacity),
        (sds(wire, BF16), sds((tok_rows, 8), F32)),
        "dispatch",
        in_specs=[HBM] * 4,
        out_specs=(VMEM, VMEM),
        scratch_shapes=[scratch(ids.shape, jnp.int32), scratch(cw.shape, F32)]
        + [scratch(tokens.shape, BF16)] * 2
        + [sems((4,))],
    )(*in_hbm(ids, cw, tokens, cotangent))
    received = lax.all_to_all(sent, "exp", split_axis=0, concat_axis=0, tiled=True)
    grads, results = call(
        experts_step,
        (pltpu.HBM((replicas, 3, part, ff), BF16), pltpu.HBM(wire, BF16)),
        "experts_step",
        in_specs=[VMEM, HBM],
        out_specs=(HBM, HBM),
        scratch_shapes=[
            scratch((3, replicas, part, ff), BF16),
            scratch((3, replicas, part, ff), BF16),
            scratch(wire, BF16),
        ]
        + [scratch((rows, ff), BF16)] * 3
        + [sems((3,)), sems((3, 2)), sems((2, 2))],
    )(received, *in_hbm(weights))
    grads = grads.reshape(replicas * 3 * part, ff)
    reduced = lax.psum_scatter(grads, "rep", scatter_dimension=0, tiled=True)
    reduced = reduced.reshape(3, part, ff)
    back = lax.all_to_all(results, "exp", split_axis=0, concat_axis=0, tiled=True)
    mixed, token_grad = call(
        combine,
        (pltpu.HBM((tok_rows, features), BF16),) * 2,
        "combine",
        in_specs=[VMEM, VMEM],
        out_specs=(HBM, HBM),
        scratch_shapes=[scratch((tok_rows, features), BF16)] * 2 + [sems((2,))],
    )(table, back)
    gate_grad, up_grad, down_grad = call(
        average_grads(replicas),
        (pltpu.HBM((part, ff), BF16), pltpu.HBM((part, ff), BF16), pltpu.HBM((ff, part), BF16)),
        "average_grads",
        in_specs=[HBM],
        out_specs=(HBM,) * 3,
        scratch_shapes=[
            scratch((3, part, ff), BF16),
            scratch((2, part, ff), BF16),
            scratch((ff, part), BF16),
            sems((3,)),
            sems((3,)),
        ],
    )(*in_hbm(reduced))
    return (mixed, token_grad, gate_grad[None], up_grad[None], down_grad[None])


def solution(mesh):
    placed = (
        P(("rep", "exp"), None),
        P(("rep", "exp"), None),
        P(("rep", "exp"), None),
        P(("rep", "exp"), None),
        P("exp", "rep", None),
        P("exp", "rep", None),
        P("exp", None, "rep"),
    )
    return jax.shard_map(
        per_device,
        mesh=mesh,
        in_specs=placed,
        out_specs=(
            P(("rep", "exp"), None),
            P(("rep", "exp"), None),
            P("exp", "rep", None),
            P("exp", "rep", None),
            P("exp", None, "rep"),
        ),
        check_vma=False,
    )
```
